32 devices in a mesh: groups: 2 (over y), seq: 4 (over z), chan: 4 (over x, core).
Axes of the slice: x: 2, y: 2, z: 4, core: 2. Of those that a mesh axis runs over, the one named last changes fastest.
Arguments:
- x_in: bfloat16 [3072, 8192], P(('groups', 'seq'), 'chan'), parts along dimension 0, may hold values from -6 to 6
- b_in: bfloat16 [3072, 8, 128], P(('groups', 'seq'), 'chan'), parts along dimension 0, may hold values from -6 to 6
- c_in: bfloat16 [3072, 8, 128], P(('groups', 'seq'), 'chan'), parts along dimension 0, may hold values from -6 to 6
- dt_in: float32 [3072, 128], P(('groups', 'seq'), 'chan'), parts along dimension 0, may hold values from -1.1 to 3.3
- a_log: float32 [128], P('chan'), may hold values from -11 to -3.4
- z_in: bfloat16 [3072, 8192], P(('groups', 'seq'), 'chan'), parts along dimension 0, may hold values from -6 to 6
- conv_x: float32 [4, 8192], P(None, 'chan'), may hold values from -3 to 3
- conv_bc: float32 [2, 4, 8, 128], P(None, None, 'chan'), may hold values from -3 to 3
- norm_gain: float32 [8192], P('chan'), may hold values from 0.25 to 1.75
- w_kv: bfloat16 [8192, 8, 256], P('chan'), may hold values from -1 to 1
- queries: bfloat16 [3072, 64, 128], P(('groups', 'seq'), 'chan'), parts along dimension 0, may hold values from -40 to 40
Outputs:
- mixer_out: bfloat16 [3072, 8192], P(('groups', 'seq'), 'chan'), parts along dimension 0
- attn_out: bfloat16 [3072, 64, 128], P(('groups', 'seq'), 'chan'), parts along dimension 0
The draws below stay inside these ranges and needn't reach their ends.
There are 2 independent parts, one for each index of `groups`. The reference program is written for one: setup_inputs(seed, part) draws one part's arguments, and reference() takes and returns one part's arrays. A program takes and returns all parts, laid end to end along the dimension named above; an argument that names none is the same for every part. Nothing has to cross between parts.
All inputs are finite; a program needn't handle non-finite values.
Results may differ from the reference program's by a relative error of at most 0.0045.
Values may be sent and summed in bfloat16 or wider, within the bound.
No kernel may reach another device: no remote copies, remote signals or barrier semaphores. Data moves between devices by JAX's collectives and lax.ppermute only.
A program may use at most 64 MiB of HBM per device.

```python
import math
import jax
import jax.numpy as jnp
from jax import lax

TOK_DEV = 384
D_INNER = 8192
HEADS = 128
STATE = 128
BC_GROUPS = 8
CONV = 4
STRETCH = 128
Q_HEADS = 64
KV_HEADS = 8
ATT_DIM = 128
HEAD_DIM = 64
TOKENS = 1536


def draw_dt_in(key, part):
    key_level, key_rough = jax.random.split(jax.random.fold_in(key, 11))
    blocks = TOKENS // TOK_DEV
    level = jnp.exp(jax.random.uniform(key_level, (blocks, 1, 1), jnp.float32, math.log(0.5), math.log(2.0)))
    rough = jax.random.uniform(key_rough, (blocks, TOK_DEV, HEADS), jnp.float32, -0.5, 0.5)
    step_sizes = (level * jnp.exp(rough)).reshape(TOKENS, HEADS)
    return step_sizes + jnp.log(-jnp.expm1(-step_sizes))


def draw_a_log(key, part):
    key_pick, key_fast, key_slow = jax.random.split(jax.random.fold_in(key, 23), 3)
    share = 0.5
    quick = jax.random.uniform(key_pick, (HEADS,), jnp.float32) < share
    fast_rates = jax.random.uniform(key_fast, (HEADS,), jnp.float32, math.log(1.0 / 50.0), math.log(1.0 / 30.0))
    slow_rates = jax.random.uniform(key_slow, (HEADS,), jnp.float32, math.log(0.25), math.log(0.6)) - math.log(TOKENS)
    return jnp.where(quick, fast_rates, slow_rates)


def draw_w_kv(key, part):
    key_scale, key_base = jax.random.split(jax.random.fold_in(key, 31))
    key_scales = jnp.exp(jax.random.uniform(key_scale, (KV_HEADS, ATT_DIM), jnp.float32, math.log(0.3), math.log(3.0)))
    column_scales = jnp.concatenate([key_scales, jnp.ones((KV_HEADS, ATT_DIM), jnp.float32)], axis=-1)
    shape = (D_INNER, KV_HEADS, 2 * ATT_DIM)
    base = jnp.clip(jax.random.normal(key_base, shape, jnp.float32), -4.0, 4.0)
    return (base * column_scales * D_INNER ** (-0.5)).astype(jnp.bfloat16)


def draw_queries(key, part):
    key_width, key_row, key_base = jax.random.split(jax.random.fold_in(key, 37), 3)
    width_scale = jnp.exp(jax.random.uniform(key_width, (Q_HEADS, ATT_DIM), jnp.float32, 0.0, math.log(10.0)))
    row_scale = jnp.exp(jax.random.uniform(key_row, (TOKENS, 1, 1), jnp.float32, math.log(0.1), 0.0))
    shape = (TOKENS, Q_HEADS, ATT_DIM)
    base = jnp.clip(jax.random.normal(key_base, shape, jnp.float32), -4.0, 4.0)
    return (base * width_scale * row_scale).astype(jnp.bfloat16)


def block_levels(stream_key, dims, cuts, least, largest):
    loudness = 1.0
    for axis_at, parts in cuts:
        steps = jax.random.uniform(jax.random.fold_in(jax.random.fold_in(stream_key, 6), axis_at), (parts,), jnp.float32, least / len(cuts), largest / len(cuts))
        loudness = loudness * jnp.repeat(jnp.exp(steps), dims[axis_at] // parts).reshape((-1,) + (1,) * (len(dims) - 1 - axis_at))
    return loudness


def noise(own_key, shape, width, limit, cuts=(), kind=jnp.bfloat16):
    values = jax.random.normal(own_key, shape, jnp.float32) * width
    if len(cuts) > 0:
        values = block_levels(own_key, shape, cuts, -0.22, 0.18) * values
    return jnp.clip(values, min=-limit, max=limit).astype(kind)


def setup_inputs(seed: int = 0, part: int = 0) -> dict:
    key_list = jax.random.split(jax.random.key(seed), 12)
    part_splits = jax.random.split(jax.random.fold_in(key_list[11], part), 12)
    x_in = noise(part_splits[0], (TOKENS, D_INNER), 1.0, 6.0, ((0, 4), (1, 4)))
    b_in = noise(part_splits[1], (TOKENS, BC_GROUPS, STATE), 1.0, 6.0, ((0, 4), (1, 4)))
    c_in = noise(part_splits[2], (TOKENS, BC_GROUPS, STATE), 1.0, 6.0, ((0, 4), (1, 4)))
    dt_in = draw_dt_in(jax.random.fold_in(jax.random.fold_in(key_list[11], part), 71), part)
    a_log = draw_a_log(jax.random.fold_in(key_list[11], 71), part)
    z_in = noise(part_splits[5], (TOKENS, D_INNER), 1.0, 6.0, ((0, 4), (1, 4)))
    conv_x = noise(key_list[6], (CONV, D_INNER), 0.5, 3.0, ((1, 4),), jnp.float32)
    conv_bc = noise(key_list[7], (2, CONV, BC_GROUPS, STATE), 0.5, 3.0, ((2, 4),), jnp.float32)
    norm_gain = jnp.clip(1.0 + 0.15 * jax.random.normal(key_list[8], (D_INNER,), jnp.float32), 0.25, 1.75)
    w_kv = draw_w_kv(jax.random.fold_in(key_list[11], 71), part)
    queries = draw_queries(jax.random.fold_in(jax.random.fold_in(key_list[11], part), 71), part)
    return dict(x_in=x_in, b_in=b_in, c_in=c_in, dt_in=dt_in, a_log=a_log, z_in=z_in, conv_x=conv_x, conv_bc=conv_bc, norm_gain=norm_gain, w_kv=w_kv, queries=queries)


HIGHEST = lax.Precision.HIGHEST

def silu_of(values):
    return values * jax.nn.sigmoid(values)

def rounded(values):
    return lax.optimization_barrier(values.astype(jnp.bfloat16))

def causal_conv(extended, conv_taps, token_count):
    summed = jnp.zeros((token_count,) + extended.shape[1:], jnp.float32)
    for offset in range(conv_taps.shape[0]):
        summed = summed + conv_taps[offset] * extended[offset:offset + token_count]
    return summed

def stretch_scan(x_heads, b_rows, c_rows, step_rows, decay_rates, initial):
    length = STRETCH
    blocks = x_heads.shape[0] // length
    causal_mask = (jnp.arange(length)[:, None] >= jnp.arange(length)[None, :])[:, :, None, None]

    def advance(carried, pieces):
        x_block, b_block, c_block, step_block = pieces
        running = jnp.cumsum(-step_block * decay_rates, axis=0)
        spread = running[:, None] - running[None, :]
        decays = jnp.where(causal_mask, jnp.exp(jnp.where(causal_mask, spread, 0.0)), 0.0)
        intersection = jnp.einsum('tgn,sgn->tsg', c_block, b_block, precision=HIGHEST)
        mixing = decays * intersection[..., None] * step_block[None]
        within = jnp.einsum('tsgh,sghp->tghp', mixing, x_block, precision=HIGHEST)
        before = jnp.einsum('tgn,ghpn->tghp', c_block, carried, precision=HIGHEST) * jnp.exp(running)[..., None]
        tail_weight = jnp.exp(running[-1][None] - running) * step_block
        carried = carried * jnp.exp(running[-1])[..., None, None] + jnp.einsum('sgh,sghp,sgn->ghpn', tail_weight, x_block, b_block, precision=HIGHEST)
        return (carried, within + before)

    def to_blocks(values_in):
        return values_in.reshape((blocks, length) + values_in.shape[1:])
    last_state, outputs = lax.scan(advance, initial, (to_blocks(x_heads), to_blocks(b_rows), to_blocks(c_rows), to_blocks(step_rows)))
    return (outputs.reshape(x_heads.shape), last_state)

def reference(x_in, b_in, c_in, dt_in, a_log, z_in, conv_x, conv_bc, norm_gain, w_kv, queries):
    margin = CONV - 1
    per_group = HEADS // BC_GROUPS

    def padded(values_in):
        zeros = jnp.zeros((margin,) + values_in.shape[1:], jnp.float32)
        return jnp.concatenate([zeros, values_in.astype(jnp.float32)], axis=0)
    x_conv = rounded(silu_of(causal_conv(padded(x_in), conv_x, TOKENS)))
    b_conv = rounded(silu_of(causal_conv(padded(b_in), conv_bc[0], TOKENS)))
    c_conv = rounded(silu_of(causal_conv(padded(c_in), conv_bc[1], TOKENS)))
    step_sizes = jax.nn.softplus(dt_in).reshape(TOKENS, BC_GROUPS, per_group)
    decay_rates = jnp.exp(a_log).reshape(BC_GROUPS, per_group)
    x_heads = x_conv.astype(jnp.float32).reshape(TOKENS, BC_GROUPS, per_group, HEAD_DIM)
    initial = jnp.zeros((BC_GROUPS, per_group, HEAD_DIM, STATE), jnp.float32)
    ssm_out, last_state = stretch_scan(x_heads, b_conv.astype(jnp.float32), c_conv.astype(jnp.float32), step_sizes, decay_rates, initial)
    gated_out = ssm_out.reshape(TOKENS, D_INNER) * silu_of(z_in.astype(jnp.float32))
    grouped = gated_out.reshape(TOKENS, BC_GROUPS, D_INNER // BC_GROUPS)
    normed = grouped * lax.rsqrt(lax.optimization_barrier(jnp.mean(grouped * grouped, axis=-1, keepdims=True)) + 1e-05)
    mixer_out = (normed.reshape(TOKENS, D_INNER) * norm_gain).astype(jnp.bfloat16)
    key_values = jnp.dot(mixer_out, w_kv.reshape(D_INNER, -1), preferred_element_type=jnp.float32)
    key_values = key_values.reshape(TOKENS, KV_HEADS, 2 * ATT_DIM)
    keys_raw = key_values[..., :ATT_DIM]
    key_hat = rounded(keys_raw * lax.rsqrt(lax.optimization_barrier(jnp.mean(keys_raw * keys_raw, axis=-1, keepdims=True)) + 1e-06)).astype(jnp.float32)
    value_b = rounded(key_values[..., ATT_DIM:]).astype(jnp.float32)
    query_f = queries.astype(jnp.float32)
    query_hat = rounded(query_f * lax.rsqrt(lax.optimization_barrier(jnp.mean(query_f * query_f, axis=-1, keepdims=True)) + 1e-06)).astype(jnp.float32)
    group_size = Q_HEADS // KV_HEADS
    query_hat = query_hat.reshape(TOKENS, KV_HEADS, group_size, ATT_DIM)
    query_block = math.gcd(TOKENS, 64)
    key_positions = jnp.arange(TOKENS)
    score_scale = ATT_DIM ** (-0.5)

    def attend_block(block_index):
        first_row = block_index * query_block
        query_rows = lax.dynamic_slice_in_dim(query_hat, first_row, query_block, 0)
        scores = jnp.einsum('tkga,jka->tkgj', query_rows, key_hat, precision=HIGHEST) * score_scale
        query_positions = first_row + jnp.arange(query_block)
        allowed = (query_positions[:, None] >= key_positions[None, :])[:, None, None, :]
        weights = jnp.where(allowed, jnp.exp(scores), 0.0)
        weights_b = rounded(weights).astype(jnp.float32)
        numerator = jnp.einsum('tkgj,jka->tkga', weights_b, value_b, precision=HIGHEST)
        denominator = lax.optimization_barrier(jnp.sum(weights, axis=-1))
        return (numerator / denominator[..., None]).astype(jnp.bfloat16).reshape(query_block, Q_HEADS, ATT_DIM)
    attended = lax.map(attend_block, jnp.arange(TOKENS // query_block))
    attn_out = attended.reshape(TOKENS, Q_HEADS, ATT_DIM)
    return (mixer_out, attn_out)
```

```python
import functools

import jax
import jax.numpy as jnp
from jax import lax
from jax.experimental import pallas as pl
from jax.experimental.pallas import tpu as pltpu
from jax.sharding import PartitionSpec as P

F32 = jnp.float32
BF16 = jnp.bfloat16
RIM = 8
LANES = 128


def mm(a, b):
    return lax.dot_general(a, b, (((1,), (0,)), ((), ())), preferred_element_type=F32)


def mm_nt(a, b):
    return lax.dot_general(a, b, (((1,), (1,)), ((), ())), preferred_element_type=F32)


def split2(v):
    hi = v.astype(BF16)
    lo = (v - hi.astype(F32)).astype(BF16)
    return hi, lo


def split3(v):
    hi = v.astype(BF16)
    rest = v - hi.astype(F32)
    mid = rest.astype(BF16)
    lo = (rest - mid.astype(F32)).astype(BF16)
    return hi, mid, lo


def silu(v):
    return v / (1.0 + jnp.exp(-v))


def lower_mask(rows, cols, row0=0):
    at_row = lax.broadcasted_iota(jnp.int32, (rows, cols), 0) + row0
    at_col = lax.broadcasted_iota(jnp.int32, (rows, cols), 1)
    return at_row >= at_col


def expander(heads, width, first_head, head_width):
    at_head = lax.broadcasted_iota(jnp.int32, (heads, width), 0)
    at_chan = lax.broadcasted_iota(jnp.int32, (heads, width), 1)
    low = (at_head - first_head) * head_width
    return ((at_chan >= low) & (at_chan < low + head_width)).astype(BF16)


def vmem(*shape_dtype):
    return pl.BlockSpec(memory_space=pltpu.VMEM)


def params(mib):
    return pltpu.CompilerParams(vmem_limit_bytes=mib << 20)


def conv_tile(scr, rim, body, taps, tokens):
    count = taps.shape[0]
    scr[0:RIM, :] = rim
    scr[RIM : RIM + tokens, :] = body
    total = taps[0:1, :] * scr[RIM - count + 1 : RIM - count + 1 + tokens, :]
    for j in range(1, count):
        start = RIM - count + 1 + j
        total = total + taps[j : j + 1, :] * scr[start : start + tokens, :]
    return silu(total)


def state_kernel(
    group, head_width, x_ref, xrim_ref, b_ref, brim_ref, dt_ref, alog_ref, cx_ref, cb_ref,
    sb_ref, sf_ref, xhi_ref, xlo_ref, bc_ref, e2_ref, dec_ref, scr, e1_scr,
):
    tokens, width = x_ref.shape
    heads = dt_ref.shape[1]
    per_group = width // head_width
    dt = dt_ref[...]
    steps = jnp.maximum(dt, 0.0) + jnp.log1p(jnp.exp(-jnp.abs(dt)))
    fall = -steps * jnp.exp(alog_ref[...])
    tri = lower_mask(tokens, tokens).astype(BF16)
    running = sum(mm(tri, part) for part in split3(fall))
    e2 = jnp.exp(running)
    e2_ref[...] = e2
    e1_hi, e1_lo = split2(jnp.exp(-running) * steps)
    spread = expander(heads, width, group * per_group, head_width)
    e1_scr[...] = mm(e1_hi, spread) + mm(e1_lo, spread)
    last = jnp.broadcast_to(e2[tokens - 1 : tokens, :], (8, heads))
    dec = sum(mm(part, spread) for part in split3(last))
    dec_ref[...] = dec
    bc = conv_tile(scr, brim_ref[...].astype(F32), b_ref[...].astype(F32), cb_ref[...], tokens).astype(BF16)
    bc_ref[...] = bc
    bct = bc.astype(F32).T.astype(BF16)

    def column(i, _):
        cols = pl.ds(pl.multiple_of(i * LANES, LANES), LANES)
        xc = conv_tile(scr, xrim_ref[:, cols].astype(F32), x_ref[:, cols].astype(F32), cx_ref[:, cols], tokens)
        xs = xc.astype(BF16).astype(F32) * e1_scr[:, cols]
        hi, lo = split2(xs)
        xhi_ref[:, cols] = hi
        xlo_ref[:, cols] = lo
        return 0

    lax.fori_loop(0, width // LANES, column, 0)
    state = (mm(bct, xhi_ref[...]) + mm(bct, xlo_ref[...])) * dec[0:1, :]
    sf_ref[...] = state
    sb_ref[...] = state.astype(BF16)


def local_kernel(
    group, head_width, c_ref, crim_ref, cc_ref, bc_ref, xhi_ref, xlo_ref, e2_ref, z_ref,
    cconv_ref, y_ref, zg_ref, scr, hi_scr, lo_scr,
):
    tokens, width = xhi_ref.shape
    heads = e2_ref.shape[1]
    per_group = width // head_width
    cc = conv_tile(scr, crim_ref[...].astype(F32), c_ref[...].astype(F32), cc_ref[...], tokens).astype(BF16)
    cconv_ref[...] = cc
    cross = jnp.where(lower_mask(tokens, tokens), mm_nt(cc, bc_ref[...]), 0.0)
    hi, lo = split2(cross)
    hi_scr[...] = hi
    lo_scr[...] = lo
    e2_hi, e2_lo = split2(e2_ref[...])
    tile = 2 * LANES

    def column(i, _):
        cols = pl.ds(pl.multiple_of(i * tile, tile), tile)
        at_head = lax.broadcasted_iota(jnp.int32, (heads, tile), 0)
        at_chan = lax.broadcasted_iota(jnp.int32, (heads, tile), 1) + i * tile
        low = (at_head - group * per_group) * head_width
        spread = ((at_chan >= low) & (at_chan < low + head_width)).astype(BF16)
        e2x = mm(e2_hi, spread) + mm(e2_lo, spread)
        zg = e2x * silu(z_ref[:, cols].astype(F32))
        xh = xhi_ref[:, cols]
        y = mm(hi_scr[...], xh) + mm(lo_scr[...], xh) + mm(hi_scr[...], xlo_ref[:, cols])
        zg_ref[:, cols] = zg
        y_ref[:, cols] = y * zg
        return 0

    lax.fori_loop(0, width // tile, column, 0)


def combine_kernel(r_ref, sf_ref, dec_ref, o_ref):
    o_ref[...] = (r_ref[...].astype(F32) * dec_ref[0:1, :] + sf_ref[...]).astype(BF16)


def post_kernel(core_ref, s_ref, cconv_ref, y_ref, zg_ref, gain_ref, w_ref, mix_ref, keep_ref, send_ref, gated, mixed, acc):
    g = pl.program_id(0)
    tokens, width = y_ref.shape
    tile = 2 * LANES
    pieces, _, piece = keep_ref.shape
    cc = cconv_ref[0]

    def column(i, total):
        cols = pl.ds(pl.multiple_of(i * tile, tile), tile)
        v = y_ref[:, cols] + zg_ref[:, cols] * mm(cc, s_ref[0, :, cols])
        gated[:, cols] = v
        return total + jnp.sum(v * v, axis=1, keepdims=True)

    total = lax.fori_loop(0, width // tile, column, jnp.zeros((tokens, 1), F32))
    scale = lax.rsqrt(total / width + 1e-05)

    def write(i, _):
        cols = pl.ds(pl.multiple_of(i * tile, tile), tile)
        m = (gated[:, cols] * scale * gain_ref[0:1, cols]).astype(BF16)
        mix_ref[:, cols] = m
        mixed[:, cols] = m
        return 0

    lax.fori_loop(0, width // tile, write, 0)

    def project(i, _):
        cols = pl.ds(pl.multiple_of(i * piece, piece), piece)
        part = mm(mixed[...], w_ref[:, cols])
        acc[:, cols] = jnp.where(g == 0, part, acc[:, cols] + part)
        return 0

    lax.fori_loop(0, acc.shape[1] // piece, project, 0)

    @pl.when(g == pl.num_programs(0) - 1)
    def _():
        core = core_ref[0]
        for x in range(pieces):
            mine = pl.multiple_of((2 * x + core) * piece, piece)
            other = pl.multiple_of((2 * x + 1 - core) * piece, piece)
            keep_ref[x] = acc[:, pl.ds(mine, piece)]
            send_ref[x] = acc[:, pl.ds(other, piece)].astype(BF16)


def chip_sum_kernel(x_ref, keep_ref, got_ref, own_ref, send_ref):
    pieces = keep_ref.shape[0]
    x = x_ref[0]
    own_ref[...] = keep_ref[x] + got_ref[x].astype(F32)
    for s in range(1, pieces):
        at = lax.rem(x + s, pieces)
        send_ref[s - 1] = (keep_ref[at] + got_ref[at].astype(F32)).astype(BF16)


def key_kernel(pieces, att, *refs):
    own_ref, out_ref = refs[0], refs[-1]
    kv = own_ref[...]
    for s in range(1, pieces):
        kv = kv + refs[s][...].astype(F32)
    for h in range(kv.shape[1] // (2 * att)):
        key = kv[:, 2 * h * att : (2 * h + 1) * att]
        scale = lax.rsqrt(jnp.mean(key * key, axis=-1, keepdims=True) + 1e-06)
        out_ref[:, 2 * h * att : (2 * h + 1) * att] = (key * scale).astype(BF16)
        out_ref[:, (2 * h + 1) * att : (2 * h + 2) * att] = kv[:, (2 * h + 1) * att : (2 * h + 2) * att].astype(BF16)


def attend_kernel(shards, kv_here, att, block, *refs):
    seq_ref, q_ref = refs[0], refs[1]
    kv_refs = refs[2 : 2 + shards]
    o_ref, acc, vext = refs[2 + shards :]
    tokens = kv_refs[0].shape[0]
    q_heads = q_ref.shape[1]
    per = q_heads // kv_here
    seq = seq_ref[0]
    factor = att ** (-0.5) * 1.4426950408889634
    rows = block * per
    for s in range(shards):
        for h in range(kv_here):
            vext[s, h, :, 0:att] = kv_refs[s][:, (2 * h + 1) * att : (2 * h + 2) * att]
            vext[s, h, :, att : 2 * att] = jnp.ones((tokens, att), BF16)
    for b in range(tokens // block):
        first = b * block
        qf = q_ref[first : first + block].astype(F32)
        outs = []
        for h in range(kv_here):
            qh = qf[:, h * per : (h + 1) * per, :].reshape(rows, att)
            qn = (qh * lax.rsqrt(jnp.mean(qh * qh, axis=-1, keepdims=True) + 1e-06)).astype(BF16)
            span = first + block
            scores = mm_nt(qn, kv_refs[0][0:span, 2 * h * att : (2 * h + 1) * att])
            at_token = lax.broadcasted_iota(jnp.int32, (block, per, span), 0).reshape(rows, span) + first
            at_key = lax.broadcasted_iota(jnp.int32, (rows, span), 1)
            wts = jnp.where(at_token >= at_key, jnp.exp2(scores * factor), 0.0).astype(BF16)
            acc[...] = mm(wts, vext[0, h, 0:span, :])
            for s in range(1, shards):

                @pl.when(seq >= s)
                def _():
                    sc = mm_nt(qn, kv_refs[s][:, 2 * h * att : (2 * h + 1) * att])
                    acc[...] += mm(jnp.exp2(sc * factor).astype(BF16), vext[s, h])

            outs.append((acc[:, 0:att] / acc[:, att : 2 * att]).reshape(block, per, att))
        o_ref[first : first + block] = jnp.concatenate(outs, axis=1).astype(BF16)


def on_device(x_in, b_in, c_in, dt_in, a_log, z_in, conv_x, conv_bc, norm_gain, w_kv, queries):
    tokens, channels = x_in.shape
    groups, state_width = b_in.shape[1:]
    heads = dt_in.shape[1]
    head_width = channels // heads
    width = channels // groups
    seq_count = lax.axis_size("seq")
    chan_count = lax.axis_size("chan")
    seq_index = lax.axis_index("seq")
    chan_index = lax.axis_index("chan")
    taps = conv_x.shape[0]
    flat = groups * state_width
    kv_all, kv_width = w_kv.shape[1:]
    att = queries.shape[2]
    kv_here = kv_all // chan_count
    piece = kv_here * kv_width
    chips = chan_count // 2

    b_flat = b_in.reshape(tokens, flat)
    c_flat = c_in.reshape(tokens, flat)
    rim = jnp.concatenate([x_in[tokens - RIM :], b_flat[tokens - RIM :], c_flat[tokens - RIM :]], axis=1)
    rim = lax.ppermute(rim, "seq", [(i, i + 1) for i in range(seq_count - 1)])
    bc_taps = conv_bc.reshape(2, taps, flat)

    def sd(shape, dtype):
        return jax.ShapeDtypeStruct(shape, dtype)

    def block(shape, *at):
        return pl.BlockSpec(shape, lambda i: at)

    state_parts = []
    for g in range(groups):
        outs = pl.pallas_call(
            functools.partial(state_kernel, g, head_width),
            grid=(1,),
            in_specs=[
                block((tokens, width), 0, g),
                block((RIM, width), 0, g),
                block((tokens, state_width), 0, g),
                block((RIM, state_width), 0, channels // state_width + g),
                block((tokens, heads), 0, 0),
                block((1, heads), 0, 0),
                block((taps, width), 0, g),
                pl.BlockSpec((None, taps, state_width), lambda i, g=g: (0, 0, g)),
            ],
            out_specs=[
                block((state_width, width), 0, 0),
                block((state_width, width), 0, 0),
                block((tokens, width), 0, 0),
                block((tokens, width), 0, 0),
                block((tokens, state_width), 0, 0),
                block((tokens, heads), 0, 0),
                block((8, width), 0, 0),
            ],
            out_shape=[
                sd((state_width, width), BF16),
                sd((state_width, width), F32),
                sd((tokens, width), BF16),
                sd((tokens, width), BF16),
                sd((tokens, state_width), BF16),
                sd((tokens, heads), F32),
                sd((8, width), F32),
            ],
            scratch_shapes=[pltpu.VMEM((RIM + tokens, LANES), F32), pltpu.VMEM((tokens, width), F32)],
            compiler_params=params(40),
            cost_estimate=pl.CostEstimate(flops=10**9, bytes_accessed=8 * 10**6, transcendentals=0),
            name=f"state_{g}",
        )(x_in, rim, b_flat, rim, dt_in, a_log.reshape(1, heads), conv_x, bc_taps)
        state_parts.append(outs)

    local_parts = []
    for g in range(groups):
        sb, sf, xhi, xlo, bc, e2, dec = state_parts[g]
        outs = pl.pallas_call(
            functools.partial(local_kernel, g, head_width),
            grid=(1,),
            in_specs=[
                block((tokens, state_width), 0, g),
                block((RIM, state_width), 0, (channels + flat) // state_width + g),
                pl.BlockSpec((None, taps, state_width), lambda i, g=g: (1, 0, g)),
                block((tokens, state_width), 0, 0),
                block((tokens, width), 0, 0),
                block((tokens, width), 0, 0),
                block((tokens, heads), 0, 0),
                block((tokens, width), 0, g),
            ],
            out_specs=[
                block((tokens, state_width), 0, 0),
                block((tokens, width), 0, 0),
                block((tokens, width), 0, 0),
            ],
            out_shape=[sd((tokens, state_width), BF16), sd((tokens, width), F32), sd((tokens, width), F32)],
            scratch_shapes=[
                pltpu.VMEM((RIM + tokens, state_width), F32),
                pltpu.VMEM((tokens, tokens), BF16),
                pltpu.VMEM((tokens, tokens), BF16),
            ],
            compiler_params=params(40),
            cost_estimate=pl.CostEstimate(flops=2 * 10**9, bytes_accessed=8 * 10**6, transcendentals=0),
            name=f"local_{g}",
        )(c_flat, rim, bc_taps, bc, xhi, xlo, e2, z_in)
        local_parts.append(outs)

    combine = pl.pallas_call(
        combine_kernel,
        out_shape=sd((state_width, width), BF16),
        in_specs=[vmem()] * 3,
        out_specs=vmem(),
        name="combine",
    )
    sums = [part[0] for part in state_parts]
    incoming = [jnp.zeros((state_width, width), BF16) for _ in range(groups)]
    for hop in range(seq_count - 1):
        for g in range(groups):
            got = lax.ppermute(sums[g], "seq", [(hop, hop + 1)])
            incoming[g] = jnp.where(seq_index == hop + 1, got, incoming[g])
            if hop < seq_count - 2:
                sums[g] = combine(got, state_parts[g][1], state_parts[g][6])

    w_flat = w_kv.reshape(channels, kv_all * kv_width)
    keep, send = None, None
    core = lax.rem(chan_index, 2).reshape(1)
    chip = (chan_index // 2).reshape(1)

    s_all = jnp.stack(incoming)
    c_all = jnp.stack([part[0] for part in local_parts])
    y_all = jnp.concatenate([part[1] for part in local_parts], axis=1)
    zg_all = jnp.concatenate([part[2] for part in local_parts], axis=1)
    mixer_out, keep, send = pl.pallas_call(
        post_kernel,
        grid_spec=pltpu.PrefetchScalarGridSpec(
            num_scalar_prefetch=1,
            grid=(groups,),
            in_specs=[
                pl.BlockSpec((1, state_width, width), lambda g, c: (g, 0, 0)),
                pl.BlockSpec((1, tokens, state_width), lambda g, c: (g, 0, 0)),
                pl.BlockSpec((tokens, width), lambda g, c: (0, g)),
                pl.BlockSpec((tokens, width), lambda g, c: (0, g)),
                pl.BlockSpec((1, width), lambda g, c: (0, g)),
                pl.BlockSpec((width, kv_all * kv_width), lambda g, c: (g, 0)),
            ],
            out_specs=[
                pl.BlockSpec((tokens, width), lambda g, c: (0, g)),
                pl.BlockSpec((chips, tokens, piece), lambda g, c: (0, 0, 0)),
                pl.BlockSpec((chips, tokens, piece), lambda g, c: (0, 0, 0)),
            ],
            scratch_shapes=[
                pltpu.VMEM((tokens, width), F32),
                pltpu.VMEM((tokens, width), BF16),
                pltpu.VMEM((tokens, kv_all * kv_width), F32),
            ],
        ),
        out_shape=[
            sd((tokens, channels), BF16),
            sd((chips, tokens, piece), F32),
            sd((chips, tokens, piece), BF16),
        ],
        compiler_params=params(56),
        name="post",
    )(core, s_all, c_all, y_all, zg_all, norm_gain.reshape(1, channels), w_flat)

    got = lax.ppermute(send, "chan", [(i, i ^ 1) for i in range(chan_count)])
    own, out_pieces = pl.pallas_call(
        chip_sum_kernel,
        grid_spec=pltpu.PrefetchScalarGridSpec(
            num_scalar_prefetch=1,
            grid=(1,),
            in_specs=[pl.BlockSpec((chips, tokens, piece), lambda i, c: (0, 0, 0))] * 2,
            out_specs=[
                pl.BlockSpec((tokens, piece), lambda i, c: (0, 0)),
                pl.BlockSpec((chips - 1, tokens, piece), lambda i, c: (0, 0, 0)),
            ],
        ),
        out_shape=[sd((tokens, piece), F32), sd((chips - 1, tokens, piece), BF16)],
        compiler_params=params(40),
        name="chip_sum",
    )(chip, keep, got)
    received = []
    for s in range(1, chips):
        pairs = [(x * 2 + k, ((x + s) % chips) * 2 + k) for x in range(chips) for k in range(2)]
        received.append(lax.ppermute(out_pieces[s - 1], "chan", pairs))
    keyval = pl.pallas_call(
        functools.partial(key_kernel, chips, att),
        out_shape=sd((tokens, piece), BF16),
        in_specs=[vmem()] * chips,
        out_specs=vmem(),
        name="keys",
    )(own, *received)

    shards = [keyval]
    for s in range(1, seq_count):
        shards.append(lax.ppermute(keyval, "seq", [(i, i + s) for i in range(seq_count - s)]))
    attn_out = pl.pallas_call(
        functools.partial(attend_kernel, seq_count, kv_here, att, LANES),
        out_shape=sd(queries.shape, BF16),
        in_specs=[pl.BlockSpec(memory_space=pltpu.SMEM)] + [vmem()] * (1 + seq_count),
        out_specs=vmem(),
        scratch_shapes=[
            pltpu.VMEM((LANES * (queries.shape[1] // kv_here), 2 * att), F32),
            pltpu.VMEM((seq_count, kv_here, tokens, 2 * att), BF16),
        ],
        compiler_params=params(56),
        name="attend",
    )(seq_index.reshape(1), queries, *shards)
    return (mixer_out, attn_out)


def solution(mesh):
    return jax.shard_map(
        on_device,
        mesh=mesh,
        in_specs=(
            P(("groups", "seq"), "chan"),
            P(("groups", "seq"), "chan", None),
            P(("groups", "seq"), "chan", None),
            P(("groups", "seq"), "chan"),
            P("chan"),
            P(("groups", "seq"), "chan"),
            P(None, "chan"),
            P(None, None, "chan", None),
            P("chan"),
            P("chan", None, None),
            P(("groups", "seq"), "chan", None),
        ),
        out_specs=(P(("groups", "seq"), "chan"), P(("groups", "seq"), "chan", None)),
        check_vma=False,
    )
```

```python
import functools

import jax
import jax.numpy as jnp
from jax import lax
from jax.experimental import pallas as pl
from jax.experimental.pallas import tpu as pltpu
from jax.sharding import PartitionSpec as P

F32 = jnp.float32
BF16 = jnp.bfloat16
RIM = 8
LANES = 128


def mm(a, b):
    return lax.dot_general(a, b, (((1,), (0,)), ((), ())), preferred_element_type=F32)


def mm_nt(a, b):
    return lax.dot_general(a, b, (((1,), (1,)), ((), ())), preferred_element_type=F32)


def mm_tn(a, b):
    return lax.dot_general(a, b, (((0,), (0,)), ((), ())), preferred_element_type=F32)


def split2(v):
    hi = v.astype(BF16)
    lo = (v - hi.astype(F32)).astype(BF16)
    return hi, lo


def split3(v):
    hi = v.astype(BF16)
    rest = v - hi.astype(F32)
    mid = rest.astype(BF16)
    lo = (rest - mid.astype(F32)).astype(BF16)
    return hi, mid, lo


def silu(v):
    return v / (1.0 + jnp.exp(-v))


def lower_mask(rows, cols, row0=0):
    at_row = lax.broadcasted_iota(jnp.int32, (rows, cols), 0) + row0
    at_col = lax.broadcasted_iota(jnp.int32, (rows, cols), 1)
    return at_row >= at_col


def mask_upper(size):
    at_row = lax.broadcasted_iota(jnp.int32, (size, size), 0)
    at_col = lax.broadcasted_iota(jnp.int32, (size, size), 1)
    return at_row <= at_col


def expander(heads, width, first_head, head_width):
    at_head = lax.broadcasted_iota(jnp.int32, (heads, width), 0)
    at_chan = lax.broadcasted_iota(jnp.int32, (heads, width), 1)
    low = (at_head - first_head) * head_width
    return ((at_chan >= low) & (at_chan < low + head_width)).astype(BF16)


def vmem(*shape_dtype):
    return pl.BlockSpec(memory_space=pltpu.VMEM)


def params(mib):
    return pltpu.CompilerParams(vmem_limit_bytes=mib << 20)


def conv_tile(scr, rim, body, taps, tokens):
    count = len(taps)
    scr[0:RIM, :] = rim
    scr[RIM : RIM + tokens, :] = body
    total = taps[0] * scr[RIM - count + 1 : RIM - count + 1 + tokens, :]
    for j in range(1, count):
        start = RIM - count + 1 + j
        total = total + taps[j] * scr[start : start + tokens, :]
    return silu(total)


def state_kernel(
    group, head_width, x_ref, xrim_ref, b_ref, brim_ref, dt_ref, alog_ref, cx_ref, cb_ref,
    sb_ref, sf_ref, xhi_ref, xlo_ref, bc_ref, e2_ref, dec_ref, scr, e1_scr,
):
    tokens, width = x_ref.shape
    heads = dt_ref.shape[0]
    per_group = width // head_width
    dt = dt_ref[...]
    steps = jnp.maximum(dt, 0.0) + jnp.log1p(jnp.exp(-jnp.abs(dt)))
    square = lax.broadcasted_iota(jnp.int32, (heads, heads), 0) == lax.broadcasted_iota(jnp.int32, (heads, heads), 1)
    rates = jnp.sum(jnp.where(square, jnp.exp(alog_ref[...]), 0.0), axis=1, keepdims=True)
    fall = -steps * rates
    upper = mask_upper(tokens).astype(BF16)
    running = sum(mm(part, upper) for part in split3(fall))
    e2 = jnp.exp(running)
    e2_ref[...] = e2
    spread = expander(heads, width, group * per_group, head_width)
    e1_hi, e1_lo = split2(jnp.exp(-running) * steps)
    e1_scr[...] = mm_tn(e1_hi, spread) + mm_tn(e1_lo, spread)
    tail = sum(mm_tn(part, spread) for part in split3(e2[:, tokens - LANES :]))
    dec = tail[LANES - 8 :, :]
    dec_ref[...] = dec
    taps = [cb_ref[0, j, group : group + 1, :] for j in range(cb_ref.shape[1])]
    bc = conv_tile(scr, brim_ref[...].astype(F32), b_ref[...].astype(F32), taps, tokens).astype(BF16)
    bc_ref[...] = bc
    bct = bc.astype(F32).T.astype(BF16)

    def column(i, _):
        cols = pl.ds(pl.multiple_of(i * LANES, LANES), LANES)
        taps = [cx_ref[j : j + 1, cols] for j in range(cx_ref.shape[0])]
        xc = conv_tile(scr, xrim_ref[:, cols].astype(F32), x_ref[:, cols].astype(F32), taps, tokens)
        xs = xc.astype(BF16).astype(F32) * e1_scr[:, cols]
        hi, lo = split2(xs)
        xhi_ref[:, cols] = hi
        xlo_ref[:, cols] = lo
        return 0

    lax.fori_loop(0, width // LANES, column, 0)
    state = (mm(bct, xhi_ref[...]) + mm(bct, xlo_ref[...])) * dec[7:8, :]
    sf_ref[...] = state
    sb_ref[...] = state.astype(BF16)


def local_kernel(
    group, head_width, c_ref, crim_ref, cc_ref, bc_ref, xhi_ref, xlo_ref, e2_ref, z_ref,
    cconv_ref, y_ref, zg_ref, scr, hi_scr, lo_scr,
):
    tokens, width = xhi_ref.shape
    heads = e2_ref.shape[0]
    per_group = width // head_width
    taps = [cc_ref[1, j, group : group + 1, :] for j in range(cc_ref.shape[1])]
    cc = conv_tile(scr, crim_ref[...].astype(F32), c_ref[...].astype(F32), taps, tokens).astype(BF16)
    cconv_ref[...] = cc
    cross = jnp.where(lower_mask(tokens, tokens), mm_nt(cc, bc_ref[...]), 0.0)
    hi, lo = split2(cross)
    hi_scr[...] = hi
    lo_scr[...] = lo
    e2_hi, e2_lo = split2(e2_ref[...])
    tile = 2 * LANES

    def column(i, _):
        cols = pl.ds(pl.multiple_of(i * tile, tile), tile)
        at_head = lax.broadcasted_iota(jnp.int32, (heads, tile), 0)
        at_chan = lax.broadcasted_iota(jnp.int32, (heads, tile), 1) + i * tile
        low = (at_head - group * per_group) * head_width
        spread = ((at_chan >= low) & (at_chan < low + head_width)).astype(BF16)
        e2x = mm_tn(e2_hi, spread) + mm_tn(e2_lo, spread)
        zg = e2x * silu(z_ref[:, cols].astype(F32))
        xh = xhi_ref[:, cols]
        y = mm(hi_scr[...], xh) + mm(lo_scr[...], xh) + mm(hi_scr[...], xlo_ref[:, cols])
        zg_ref[:, cols] = zg
        y_ref[:, cols] = y * zg
        return 0

    lax.fori_loop(0, width // tile, column, 0)


def post_kernel(s_ref, cconv_ref, y_ref, zg_ref, gain_ref, *refs):
    mix_ref, all_ref, gated = refs[-3:]
    tokens, width = y_ref.shape
    tile = 2 * LANES
    cc = cconv_ref[...]

    def column(i, total):
        cols = pl.ds(pl.multiple_of(i * tile, tile), tile)
        v = y_ref[:, cols] + zg_ref[:, cols] * mm(cc, s_ref[:, cols])
        gated[:, cols] = v
        square = v * v
        return total + square[:, :LANES] + square[:, LANES:]

    total = lax.fori_loop(0, width // tile, column, jnp.zeros((tokens, LANES), F32))
    scale = lax.rsqrt(jnp.sum(total, axis=1, keepdims=True) / width + 1e-05)

    def write(i, _):
        cols = pl.ds(pl.multiple_of(i * tile, tile), tile)
        m = (gated[:, cols] * scale * gain_ref[0:1, cols]).astype(BF16)
        mix_ref[:, cols] = m
        all_ref[:, cols] = m
        return 0

    lax.fori_loop(0, width // tile, write, 0)


def key_kernel(att, own_ref, *refs):
    out_ref = refs[-1]
    for h in range(own_ref.shape[0]):
        kv = own_ref[h]
        for ref in refs[:-1]:
            kv = kv + ref[h].astype(F32)
        key = kv[:, :att]
        scale = lax.rsqrt(jnp.mean(key * key, axis=-1, keepdims=True) + 1e-06)
        out_ref[h, :, :att] = (key * scale).astype(BF16)
        out_ref[h, :, att:] = kv[:, att:].astype(BF16)


def attend_kernel(shards, kv_here, att, block, *refs):
    seq_ref, q_ref = refs[0], refs[1]
    kv_refs = refs[2 : 2 + shards]
    o_ref, acc, vext = refs[2 + shards :]
    tokens = kv_refs[0].shape[1]
    q_heads = q_ref.shape[1]
    per = q_heads // kv_here
    seq = seq_ref[0]
    factor = att ** (-0.5) * 1.4426950408889634
    rows = block * per
    for s in range(shards):
        for h in range(kv_here):
            vext[s, h, :, 0:att] = kv_refs[s][h, :, att : 2 * att]
            vext[s, h, :, att : 2 * att] = jnp.ones((tokens, att), BF16)
    for b in range(tokens // block):
        first = b * block
        qf = q_ref[first : first + block].astype(F32)
        outs = []
        for h in range(kv_here):
            qh = qf[:, h * per : (h + 1) * per, :].reshape(rows, att)
            qn = (qh * lax.rsqrt(jnp.mean(qh * qh, axis=-1, keepdims=True) + 1e-06)).astype(BF16)
            span = first + block
            scores = mm_nt(qn, kv_refs[0][h, 0:span, :att])
            at_token = lax.broadcasted_iota(jnp.int32, (block, per, span), 0).reshape(rows, span) + first
            at_key = lax.broadcasted_iota(jnp.int32, (rows, span), 1)
            wts = jnp.where(at_token >= at_key, jnp.exp2(scores * factor), 0.0).astype(BF16)
            acc[...] = mm(wts, vext[0, h, 0:span, :])
            for s in range(1, shards):

                @pl.when(seq >= s)
                def _():
                    sc = mm_nt(qn, kv_refs[s][h, :, :att])
                    acc[...] += mm(jnp.exp2(sc * factor).astype(BF16), vext[s, h])

            outs.append((acc[:, 0:att] / acc[:, att : 2 * att]).reshape(block, per, att))
        o_ref[first : first + block] = jnp.concatenate(outs, axis=1).astype(BF16)


def on_device(x_in, b_in, c_in, dt_in, a_log, z_in, conv_x, conv_bc, norm_gain, w_kv, queries):
    tokens, channels = x_in.shape
    groups, state_width = b_in.shape[1:]
    heads = dt_in.shape[1]
    head_width = channels // heads
    width = channels // groups
    seq_count = lax.axis_size("seq")
    chan_count = lax.axis_size("chan")
    seq_index = lax.axis_index("seq")
    chan_index = lax.axis_index("chan")
    taps = conv_x.shape[0]
    flat = groups * state_width
    kv_all, kv_width = w_kv.shape[1:]
    att = queries.shape[2]
    kv_here = kv_all // chan_count
    piece = kv_here * kv_width
    chips = chan_count // 2

    b_flat, c_flat = lax.optimization_barrier((b_in.reshape(tokens, flat), c_in.reshape(tokens, flat)))
    rim = jnp.concatenate([x_in[tokens - RIM :], b_flat[tokens - RIM :], c_flat[tokens - RIM :]], axis=1)
    rim = lax.ppermute(rim, "seq", [(i, i + 1) for i in range(seq_count - 1)])

    def sd(shape, dtype):
        return jax.ShapeDtypeStruct(shape, dtype)

    def block(shape, *at):
        return pl.BlockSpec(shape, lambda i: at)

    state_parts = []
    for g in range(groups):
        outs = pl.pallas_call(
            functools.partial(state_kernel, g, head_width),
            grid=(1,),
            in_specs=[
                block((tokens, width), 0, g),
                block((RIM, width), 0, g),
                block((tokens, state_width), 0, g),
                block((RIM, state_width), 0, channels // state_width + g),
                block((heads, tokens), 0, 0),
                block((1, heads), 0, 0),
                block((taps, width), 0, g),
                block(conv_bc.shape, 0, 0, 0, 0),
            ],
            out_specs=[
                block((state_width, width), 0, 0),
                block((state_width, width), 0, 0),
                block((tokens, width), 0, 0),
                block((tokens, width), 0, 0),
                block((tokens, state_width), 0, 0),
                block((heads, tokens), 0, 0),
                block((8, width), 0, 0),
            ],
            out_shape=[
                sd((state_width, width), BF16),
                sd((state_width, width), F32),
                sd((tokens, width), BF16),
                sd((tokens, width), BF16),
                sd((tokens, state_width), BF16),
                sd((heads, tokens), F32),
                sd((8, width), F32),
            ],
            scratch_shapes=[pltpu.VMEM((RIM + tokens, LANES), F32), pltpu.VMEM((tokens, width), F32)],
            compiler_params=params(16),
            cost_estimate=pl.CostEstimate(flops=10**9, bytes_accessed=8 * 10**6, transcendentals=0),
            name=f"state_{g}",
        )(x_in, rim, b_flat, rim, dt_in.T, a_log.reshape(1, heads), conv_x, conv_bc)
        state_parts.append(outs)

    local_parts = []
    for g in range(groups):
        sb, sf, xhi, xlo, bc, e2, dec = state_parts[g]
        outs = pl.pallas_call(
            functools.partial(local_kernel, g, head_width),
            grid=(1,),
            in_specs=[
                block((tokens, state_width), 0, g),
                block((RIM, state_width), 0, (channels + flat) // state_width + g),
                block(conv_bc.shape, 0, 0, 0, 0),
                block((tokens, state_width), 0, 0),
                block((tokens, width), 0, 0),
                block((tokens, width), 0, 0),
                block((heads, tokens), 0, 0),
                block((tokens, width), 0, g),
            ],
            out_specs=[
                block((tokens, state_width), 0, 0),
                block((tokens, width), 0, 0),
                block((tokens, width), 0, 0),
            ],
            out_shape=[sd((tokens, state_width), BF16), sd((tokens, width), F32), sd((tokens, width), F32)],
            scratch_shapes=[
                pltpu.VMEM((RIM + tokens, state_width), F32),
                pltpu.VMEM((tokens, tokens), BF16),
                pltpu.VMEM((tokens, tokens), BF16),
            ],
            compiler_params=params(16),
            cost_estimate=pl.CostEstimate(flops=2 * 10**9, bytes_accessed=8 * 10**6, transcendentals=0),
            name=f"local_{g}",
        )(c_flat, rim, conv_bc, bc, xhi, xlo, e2, z_in)
        local_parts.append(outs)

    sums = [part[0] for part in state_parts]
    incoming = [jnp.zeros((state_width, width), BF16) for _ in range(groups)]
    for hop in range(seq_count - 1):
        for g in range(groups):
            got = lax.ppermute(sums[g], "seq", [(hop, hop + 1)])
            incoming[g] = jnp.where(seq_index == hop + 1, got, incoming[g])
            if hop < seq_count - 2:
                sums[g] = (got.astype(F32) * state_parts[g][6][7:8] + state_parts[g][1]).astype(BF16)

    gains = norm_gain.reshape(1, channels)
    mixer_out, kv = None, 0.0
    for g in reversed(range(groups)):
        cconv, y, zg = local_parts[g]
        given = [incoming[g], cconv, y, zg, gains] + ([] if mixer_out is None else [mixer_out])
        mixed, mixer_out = pl.pallas_call(
            post_kernel,
            grid=(1,),
            in_specs=[
                block((state_width, width), 0, 0),
                block((tokens, state_width), 0, 0),
                block((tokens, width), 0, 0),
                block((tokens, width), 0, 0),
                block((1, width), 0, g),
            ]
            + [pl.BlockSpec(memory_space=pl.ANY)] * (len(given) - 5),
            out_specs=[block((tokens, width), 0, 0), block((tokens, width), 0, g)],
            out_shape=[sd((tokens, width), BF16), sd((tokens, channels), BF16)],
            scratch_shapes=[pltpu.VMEM((tokens, width), F32)],
            input_output_aliases={5: 1} if len(given) > 5 else {},
            compiler_params=params(16),
            cost_estimate=pl.CostEstimate(flops=10**9, bytes_accessed=8 * 10**6, transcendentals=0),
            name=f"post_{g}",
        )(*given)
        kv = kv + jnp.einsum("tc,chk->htk", mixed, w_kv[g * width : (g + 1) * width], preferred_element_type=F32)

    core, chip = lax.rem(chan_index, 2), lax.div(chan_index, 2)
    kv = kv.reshape(chips, 2, kv_here, tokens, kv_width)
    keep = lax.dynamic_index_in_dim(kv, core, 1, keepdims=False)
    send = lax.dynamic_index_in_dim(kv, 1 - core, 1, keepdims=False).astype(BF16)
    got = lax.ppermute(send, "chan", [(i, i ^ 1) for i in range(chan_count)])
    sums = keep + got.astype(F32)
    received = []
    for s in range(1, chips):
        pairs = [(x * 2 + k, ((x + s) % chips) * 2 + k) for x in range(chips) for k in range(2)]
        out = lax.dynamic_index_in_dim(sums, lax.rem(chip + s, chips), 0, keepdims=False).astype(BF16)
        received.append(lax.ppermute(out, "chan", pairs))
    own = lax.dynamic_index_in_dim(sums, chip, 0, keepdims=False)
    keyval = pl.pallas_call(
        functools.partial(key_kernel, att),
        out_shape=sd((kv_here, tokens, kv_width), BF16),
        in_specs=[vmem()] * chips,
        out_specs=vmem(),
        compiler_params=params(8),
        name="keys",
    )(own, *received)

    shards = [keyval]
    for s in range(1, seq_count):
        shards.append(lax.ppermute(keyval, "seq", [(i, i + s) for i in range(seq_count - s)]))
    attn_out = pl.pallas_call(
        functools.partial(attend_kernel, seq_count, kv_here, att, LANES),
        out_shape=sd(queries.shape, BF16),
        in_specs=[pl.BlockSpec(memory_space=pltpu.SMEM)] + [vmem()] * (1 + seq_count),
        out_specs=vmem(),
        scratch_shapes=[
            pltpu.VMEM((LANES * (queries.shape[1] // kv_here), 2 * att), F32),
            pltpu.VMEM((seq_count, kv_here, tokens, 2 * att), BF16),
        ],
        compiler_params=params(32),
        name="attend",
    )(seq_index.reshape(1), queries, *shards)
    return (mixer_out, attn_out)


def solution(mesh):
    return jax.shard_map(
        on_device,
        mesh=mesh,
        in_specs=(
            P(("groups", "seq"), "chan"),
            P(("groups", "seq"), "chan", None),
            P(("groups", "seq"), "chan", None),
            P(("groups", "seq"), "chan"),
            P("chan"),
            P(("groups", "seq"), "chan"),
            P(None, "chan"),
            P(None, None, "chan", None),
            P("chan"),
            P("chan", None, None),
            P(("groups", "seq"), "chan", None),
        ),
        out_specs=(P(("groups", "seq"), "chan"), P(("groups", "seq"), "chan", None)),
        check_vma=False,
    )
```
